512 devices in a mesh: row: 8 (over y), col: 16 (over z_lo, x), layer: 4 (over z_hi, core).
Axes of the slice: x: 4, y: 8, z: 8 (z_hi: 2, z_lo: 4; z = z_hi * 4 + z_lo), core: 2. Of those that a mesh axis runs over, the one named last changes fastest.
Arguments:
- root_values: bfloat16 [128, 4, 6, 128, 128], P('col', 'layer'), may hold values from -0.5 to 0.5
- root_columns: int32 [128, 4, 6], P('col', 'layer'), may hold values from 0 to 127, as said below
- root_counts: int32 [128, 4], P('col', 'layer'), may hold values from 1 to 6, as said below
- fock_values: bfloat16 [128, 4, 6, 128, 128], P('col', 'layer'), may hold values from -0.5 to 0.5
- fock_columns: int32 [128, 4, 6], P('col', 'layer'), may hold values from 0 to 127, as said below
- fock_counts: int32 [128, 4], P('col', 'layer'), may hold values from 1 to 6, as said below
- density_values: bfloat16 [128, 4, 6, 128, 128], P('col', 'layer'), may hold values from -0.5 to 0.5
- density_columns: int32 [128, 4, 6], P('col', 'layer'), may hold values from 0 to 127, as said below
- density_counts: int32 [128, 4], P('col', 'layer'), may hold values from 1 to 6, as said below
Outputs:
- fock_slab: bfloat16 [16384, 2048], P(('col', 'layer'), 'row')
- purified_slab: bfloat16 [16384, 2048], P(('col', 'layer'), 'row')
- energy_slab: bfloat16 [16384, 2048], P(('col', 'layer'), 'row')
The draws below stay inside these ranges and needn't reach their ends.
Inputs may be any that keep to these rules, and one draw needn't show every extreme that they name: `root_columns`: for each block row i and quarter q the 6 entries are distinct block columns of quarter q; entries at k >= the count are block columns too and their values are ignored. `fock_columns`: for each block row i and quarter q the 6 entries are distinct block columns of quarter q; entries at k >= the count are block columns too and their values are ignored. `density_columns`: for each block row i and quarter q the 6 entries are distinct block columns of quarter q; entries at k >= the count are block columns too and their values are ignored. `root_counts`: some entry equals 6 in every draw. `fock_counts`: some entry equals 6 in every draw. `density_counts`: some entry equals 6 in every draw.
All inputs are finite; a program needn't handle non-finite values.
Results may differ from the reference program's by a relative error of at most 0.018.
Values may be sent and summed in bfloat16 or wider, within the bound.
No kernel may reach another device: no remote copies, remote signals or barrier semaphores. Data moves between devices by JAX's collectives and lax.ppermute only.
A program may use at most 64 MiB of HBM per device.

```python
import jax
import jax.numpy as jnp
from jax import lax

BS = 128
KQ = 6
RB = 8
NB = 128
W = 2048
N_LAYER = 4


def draw_block_columns(key):
    group_size = RB // N_LAYER
    per_quarter = NB // N_LAYER
    scores = jax.random.randint(key, (NB, N_LAYER, per_quarter), 0, 1 << 20) * per_quarter + jnp.arange(per_quarter, dtype=jnp.int32)
    chosen = jnp.argsort(scores, axis=-1)[:, :, :KQ].astype(jnp.int32)
    quarter = jnp.arange(N_LAYER, dtype=jnp.int32)[None, :, None]
    return ((chosen // group_size * N_LAYER + quarter) * group_size + chosen % group_size).astype(jnp.int32)


def draw_block_counts(key):
    level_key, count_key = jax.random.split(key)
    density = jax.random.randint(level_key, (NB, 1), 1, KQ + 1)
    counts = jax.random.randint(count_key, (NB, N_LAYER), 0, 1 << 20) % density + 1
    return counts.at[0, 0].set(KQ).astype(jnp.int32)


def draw_root_columns(key, part):
    return draw_block_columns(jax.random.fold_in(key, 11))


def draw_root_counts(key, part):
    return draw_block_counts(jax.random.fold_in(key, 12))


def draw_fock_columns(key, part):
    return draw_block_columns(jax.random.fold_in(key, 21))


def draw_fock_counts(key, part):
    return draw_block_counts(jax.random.fold_in(key, 22))


def draw_density_columns(key, part):
    return draw_block_columns(jax.random.fold_in(key, 31))


def draw_density_counts(key, part):
    return draw_block_counts(jax.random.fold_in(key, 32))


def block_levels(key, extent, shards, smallest, largest):
    gain = 1.0
    for axis_at, parts in shards:
        steps = jax.random.uniform(jax.random.fold_in(jax.random.fold_in(key, 6), axis_at), (parts,), jnp.float32, smallest / len(shards), largest / len(shards))
        gain = gain * jnp.repeat(jnp.exp(steps), extent[axis_at] // parts).reshape((-1,) + (1,) * (len(extent) - 1 - axis_at))
    return gain


def gaussian(stream_key, extent, spread, most, cuts=(), held_as=jnp.bfloat16):
    loudness = block_levels(stream_key, extent, cuts, -0.22, 0.18) if cuts else 1.0
    drawn = jax.random.normal(stream_key, extent, jnp.float32) * spread * loudness
    return jnp.minimum(jnp.maximum(drawn, -most), most).astype(held_as)


def setup_inputs(seed: int = 0) -> dict:
    streams_of = jax.random.split(jax.random.key(seed), 10)
    root_values = gaussian(streams_of[0], (NB, N_LAYER, KQ, BS, BS), BS ** -0.5, 0.5, ((0, 16), (1, 4)))
    root_columns = draw_root_columns(jax.random.fold_in(streams_of[9], 71), 0)
    root_counts = draw_root_counts(jax.random.fold_in(streams_of[9], 71), 0)
    fock_values = gaussian(streams_of[3], (NB, N_LAYER, KQ, BS, BS), BS ** -0.5, 0.5, ((0, 16), (1, 4)))
    fock_columns = draw_fock_columns(jax.random.fold_in(streams_of[9], 71), 0)
    fock_counts = draw_fock_counts(jax.random.fold_in(streams_of[9], 71), 0)
    density_values = gaussian(streams_of[6], (NB, N_LAYER, KQ, BS, BS), BS ** -0.5, 0.5, ((0, 16), (1, 4)))
    density_columns = draw_density_columns(jax.random.fold_in(streams_of[9], 71), 0)
    density_counts = draw_density_counts(jax.random.fold_in(streams_of[9], 71), 0)
    return dict(root_values=root_values, root_columns=root_columns, root_counts=root_counts, fock_values=fock_values, fock_columns=fock_columns, fock_counts=fock_counts, density_values=density_values, density_columns=density_columns, density_counts=density_counts)


def extract_slab(values, columns, counts):
    targets = jnp.arange(W // BS, dtype=jnp.int32)
    usable = jnp.arange(KQ, dtype=jnp.int32)[None, None, :] < counts[:, :, None]
    onehot = ((columns[..., None] == targets) & usable[..., None]).astype(jnp.float32)
    pieces = jnp.einsum("iqkt,iqkab->iatb", onehot, values.astype(jnp.float32))
    return pieces.reshape(NB * BS, W).astype(jnp.bfloat16)


def product(values, columns, counts, slab):
    blocks = slab.astype(jnp.float32).reshape(NB, BS, W)
    summed = jnp.zeros((NB, BS, W), jnp.float32)
    for quarter in range(N_LAYER):
        partial_value = jnp.zeros((NB, BS, W), jnp.float32)
        for slot_index in range(KQ):
            picked = jnp.take(blocks, columns[:, quarter, slot_index].astype(jnp.int32), axis=0)
            usable = (counts[:, quarter] > slot_index).astype(jnp.float32)[:, None, None]
            masked_tile = values[:, quarter, slot_index].astype(jnp.float32) * usable
            partial_value = partial_value + jnp.einsum("iab,ibw->iaw", masked_tile, picked)
        rounded = lax.optimization_barrier(partial_value.astype(jnp.bfloat16))
        summed = summed + rounded.astype(jnp.float32)
    return summed.reshape(NB * BS, W)


def reference(root_values, root_columns, root_counts, fock_values, fock_columns, fock_counts, density_values, density_columns, density_counts):
    root_slab = extract_slab(root_values, root_columns, root_counts)
    fock_inner = product(fock_values, fock_columns, fock_counts, root_slab).astype(jnp.bfloat16)
    fock_slab = product(root_values, root_columns, root_counts, fock_inner).astype(jnp.bfloat16)
    density_slab = extract_slab(density_values, density_columns, density_counts)
    squared = product(density_values, density_columns, density_counts, density_slab).astype(jnp.bfloat16)
    cubed_term = product(density_values, density_columns, density_counts, squared)
    purified_slab = (3.0 * squared.astype(jnp.float32) - 2.0 * cubed_term).astype(jnp.bfloat16)
    energy_slab = product(density_values, density_columns, density_counts, fock_slab).astype(jnp.bfloat16)
    return (fock_slab, purified_slab, energy_slab)
```

```python
import functools

import jax
import jax.numpy as jnp
from jax import lax
from jax.experimental import pallas as pl
from jax.experimental.pallas import tpu as pltpu
from jax.sharding import Mesh
from jax.sharding import PartitionSpec as P

BS = 128
KQ = 6
RB = 8
HALF = RB // 2
META = KQ + 1
ROOT, FOCK, DENSITY = range(3)
COL = ("zl", "x")
LAYER = ("zh", "c")


def swapped(value, axis):
    return lax.ppermute(value, axis, [(0, 1), (1, 0)])


def extract_kernel(mat, own_meta, other_meta, place, own, other, out):
    row = place[0] + pl.program_id(0)
    start = (mat * RB + row) * META
    out[...] = jnp.zeros_like(out)
    for meta, tiles in ((own_meta, own), (other_meta, other)):
        count = meta[start + KQ]
        for k in range(KQ):

            @pl.when((meta[start + k] == place[1]) & (k < count))
            def _(k=k, tiles=tiles):
                out[0] = tiles[0, k].astype(out.dtype)


def product_kernel(mat, own_meta, other_meta, place, own, other, slab, out):
    row = place[0] + pl.program_id(0)
    start = (mat * RB + row) * META
    left, right = [], []
    for meta, tiles in ((own_meta, own), (other_meta, other)):
        count = meta[start + KQ]
        for k in range(KQ):
            j = meta[start + k]
            at = (((j >> 3) & 3) * 4 + (j >> 5)) * HALF + (j & 3)
            tile = tiles[0, k]
            left.append(jnp.where(k < count, tile, jnp.zeros_like(tile)))
            right.append(slab[at])
    total = jnp.dot(
        jnp.concatenate(left, axis=1),
        jnp.concatenate(right, axis=0),
        preferred_element_type=jnp.float32,
    )
    out[0] = total.astype(out.dtype)


def rows_call(kernel, place, metas, tiles, slab, dtype, count=HALF):
    tile_spec = pl.BlockSpec((1, KQ, BS, BS), lambda r, a, b, p: (p[0] + r, 0, 0, 0))
    slabs = [] if slab is None else [slab]
    return pl.pallas_call(
        kernel,
        out_shape=jax.ShapeDtypeStruct((count, BS, BS), dtype),
        grid_spec=pltpu.PrefetchScalarGridSpec(
            num_scalar_prefetch=3,
            grid=(count,),
            in_specs=[tile_spec, tile_spec]
            + [pl.BlockSpec(memory_space=pltpu.VMEM) for _ in slabs],
            out_specs=pl.BlockSpec((1, BS, BS), lambda r, a, b, p: (r, 0, 0)),
        ),
        cost_estimate=pl.CostEstimate(
            flops=2 * count * 2 * KQ * BS * BS * BS,
            bytes_accessed=count * 2 * KQ * BS * BS * 2,
            transcendentals=0,
        ),
    )(metas[0], metas[1], place, *tiles, *slabs)


def halves_exchanged(rows, places):
    sent = rows(places[1], jnp.bfloat16)
    arrived = swapped(sent, "zh")
    kept = rows(places[0], jnp.float32)
    return kept + arrived.astype(jnp.float32)


def gathered(piece):
    along_z = lax.all_gather(piece, "zl", axis=0, tiled=True)
    copies = jnp.broadcast_to(along_z[None], (4, *along_z.shape))
    return lax.all_to_all(copies, "x", split_axis=0, concat_axis=0, tiled=True).reshape(-1, BS, BS)


def widened(pieces):
    core = lax.axis_index("c")
    split = jnp.stack(pieces).reshape(len(pieces), 2, 2 * BS, BS)
    mine = lax.dynamic_index_in_dim(split, core, 1, keepdims=False)
    other = swapped(lax.dynamic_index_in_dim(split, 1 - core, 1, keepdims=False), "c")
    first = jnp.where(core == 0, mine, other)
    second = jnp.where(core == 0, other, mine)
    return jnp.concatenate([first, second], axis=-1)


def on_device(
    root_values,
    root_columns,
    root_counts,
    fock_values,
    fock_columns,
    fock_counts,
    density_values,
    density_columns,
    density_counts,
):
    row, zh, core = (lax.axis_index(a) for a in ("row", "zh", "c"))
    target = row * 2 + core
    places = [jnp.stack([half * HALF, target]).astype(jnp.int32) for half in (zh, 1 - zh)]
    own_meta = jnp.stack(
        [
            jnp.concatenate([columns[:, 0], counts], axis=1)
            for columns, counts in (
                (root_columns, root_counts),
                (fock_columns, fock_counts),
                (density_columns, density_counts),
            )
        ]
    ).reshape(-1)
    metas = (own_meta, swapped(own_meta, "c"))
    held = []
    for values in (root_values, fock_values, density_values):
        tiles = values[:, 0]
        held.append((tiles, swapped(tiles, "c")))

    def extracted(mat):
        def rows(place, dtype):
            kernel = functools.partial(extract_kernel, mat)
            return rows_call(kernel, place, metas, held[mat], None, dtype)

        return halves_exchanged(rows, places).astype(jnp.bfloat16)

    def product(mat, slab):
        def rows(place, dtype):
            kernel = functools.partial(product_kernel, mat)
            return rows_call(kernel, place, metas, held[mat], slab, dtype)

        return halves_exchanged(rows, places)

    root_slab = extracted(ROOT)
    density_slab = extracted(DENSITY)
    fock_inner = product(FOCK, gathered(root_slab)).astype(jnp.bfloat16)
    squared = product(DENSITY, gathered(density_slab)).astype(jnp.bfloat16)
    fock_slab = product(ROOT, gathered(fock_inner)).astype(jnp.bfloat16)
    cubed_term = product(DENSITY, gathered(squared))
    purified = (3.0 * squared.astype(jnp.float32) - 2.0 * cubed_term).astype(jnp.bfloat16)
    outs = widened([fock_slab, purified])

    all_rows = jnp.stack([jnp.int32(0), target]).astype(jnp.int32)
    partial_value = rows_call(
        functools.partial(product_kernel, DENSITY),
        all_rows,
        metas,
        held[DENSITY],
        gathered(fock_slab),
        jnp.bfloat16,
        RB,
    )
    pieces = partial_value.reshape(4, 2 * BS, BS)
    arrived = lax.all_to_all(pieces, LAYER, split_axis=0, concat_axis=0, tiled=True)
    energy = arrived.reshape(2, 2, 2 * BS, BS).astype(jnp.float32).sum(axis=0)
    energy = jnp.concatenate([energy[0], energy[1]], axis=-1).astype(jnp.bfloat16)
    return outs[0], outs[1], energy


def solution(mesh):
    finer = Mesh(mesh.devices.reshape(mesh.shape["row"], 4, 4, 2, 2), ("row", *COL, *LAYER))
    specs = (P(COL, LAYER, None, None, None), P(COL, LAYER, None), P(COL, LAYER))
    return jax.shard_map(
        on_device,
        mesh=finer,
        in_specs=specs * 3,
        out_specs=(P((*COL, *LAYER), "row"),) * 3,
        check_vma=False,
    )
```

```python
import functools

import jax
import jax.numpy as jnp
from jax import lax
from jax.experimental import pallas as pl
from jax.experimental.pallas import tpu as pltpu
from jax.sharding import Mesh
from jax.sharding import PartitionSpec as P


BS = 128
KQ = 6
RB = 8
HALF = RB // 2
META = KQ + 1
VMEM = 12 << 20
SMALL = 4 << 20
COL = ("zl", "x")
LAYER = ("zh", "c")


def swapped(value, axis):
    return lax.ppermute(value, axis, [(0, 1), (1, 0)])


def spread(value, axis):
    return lax.all_to_all(value, axis, split_axis=0, concat_axis=0, tiled=True)


def extract_kernel(mat, count, own_meta, other_meta, place, own, other, out, found, sems):
    def slot(meta, row):
        at, hit = jnp.int32(0), jnp.int32(0)
        listed = meta[(mat * META + KQ) * RB + row]
        for k in range(KQ):
            here = (meta[(mat * META + k) * RB + row] == place[1]) & (k < listed)
            at = jnp.where(here, k, at)
            hit = jnp.where(here, 1, hit)
        return at, hit

    copies, hits = [], []
    for r in range(count):
        row = place[0] + r
        for side, (meta, tiles) in enumerate(((own_meta, own), (other_meta, other))):
            at, hit = slot(meta, row)
            copy = pltpu.make_async_copy(tiles.at[row, at], found.at[r, side], sems.at[r, side])
            copy.start()
            copies.append(copy)
            hits.append(hit)
    for r in range(count):
        copies[2 * r].wait()
        copies[2 * r + 1].wait()
        zero = jnp.zeros((BS, BS), found.dtype)
        tile = jnp.where(hits[2 * r] > 0, found[r, 0], zero)
        out[r] = jnp.where(hits[2 * r + 1] > 0, found[r, 1], tile).astype(out.dtype)


def product_kernel(mat, count, own_meta, other_meta, place, own, other, slab, out):
    for r in range(count):
        row = place[0] + r
        left, right = [], []
        for meta, tiles in ((own_meta, own), (other_meta, other)):
            listed = meta[(mat * META + KQ) * RB + row]
            for k in range(KQ):
                j = meta[(mat * META + k) * RB + row]
                tile = tiles[row, k]
                left.append(jnp.where(k < listed, tile, jnp.zeros_like(tile)))
                right.append(slab[(((j >> 3) & 3) * 4 + (j >> 5)) * HALF + (j & 3)])
        total = jnp.dot(
            jnp.concatenate(left, axis=1),
            jnp.concatenate(right, axis=0),
            preferred_element_type=jnp.float32,
        )
        out[r] = total.astype(out.dtype)


def local_call(kernel, place, metas, operands, space, count, dtype, scratch):
    return pl.pallas_call(
        kernel,
        out_shape=jax.ShapeDtypeStruct((count, BS, BS), dtype),
        in_specs=[pl.BlockSpec(memory_space=pltpu.SMEM)] * 3
        + [pl.BlockSpec(memory_space=space) for _ in operands],
        out_specs=pl.BlockSpec(memory_space=pltpu.VMEM),
        scratch_shapes=scratch,
        compiler_params=pltpu.CompilerParams(vmem_limit_bytes=VMEM),
        cost_estimate=pl.CostEstimate(
            flops=2 * count * 2 * KQ * BS * BS * BS,
            bytes_accessed=count * 2 * KQ * BS * BS * 2,
            transcendentals=0,
        ),
    )(*metas, place, *operands)


def extracted(mat, metas, held, place, count, dtype):
    scratch = [pltpu.VMEM((count, 2, BS, BS), jnp.bfloat16), pltpu.SemaphoreType.DMA((count, 2))]
    kernel = functools.partial(extract_kernel, mat, count)
    return local_call(kernel, place, metas, held, pl.ANY, count, dtype, scratch)


def multiplied(mat, slab, metas, held, place, count, dtype):
    kernel = functools.partial(product_kernel, mat, count)
    return local_call(kernel, place, metas, [*held, slab], pltpu.VMEM, count, dtype, [])


def add_kernel(kept, arrived, out):
    out[...] = (kept[...] + arrived[...].astype(jnp.float32)).astype(out.dtype)


def copies_kernel(piece, out, sems):
    copies = [pltpu.make_async_copy(piece, out.at[i], sems.at[i]) for i in range(4)]
    for copy in copies:
        copy.start()
    for copy in copies:
        copy.wait()


def small_call(kernel, operands, shape, space, scratch, dtype=jnp.bfloat16):
    return pl.pallas_call(
        kernel,
        out_shape=jax.ShapeDtypeStruct(shape, dtype),
        in_specs=[pl.BlockSpec(memory_space=pltpu.VMEM) for _ in operands],
        out_specs=pl.BlockSpec(memory_space=space),
        scratch_shapes=scratch,
        compiler_params=pltpu.CompilerParams(vmem_limit_bytes=SMALL),
    )(*operands)


def exchanged(rows, places, dtype=jnp.bfloat16):
    sent = rows(places[1], HALF, jnp.bfloat16)
    arrived = swapped(sent, "zh")
    kept = rows(places[0], HALF, jnp.float32)
    return small_call(add_kernel, [kept, arrived], kept.shape, pltpu.VMEM, [], dtype)


def gathered_z(piece):
    return lax.all_gather(piece, "zl", axis=0, tiled=True)


def gathered_x(along_z):
    sems = [pltpu.SemaphoreType.DMA((4,))]
    copies = small_call(copies_kernel, [along_z], (4, *along_z.shape), pl.ANY, sems)
    return spread(copies, "x").reshape(-1, BS, BS)


def all_columns(pieces):
    core = lax.axis_index("c")
    split = jnp.stack(pieces).reshape(len(pieces), 2, 2 * BS, BS)
    mine = lax.dynamic_index_in_dim(split, core, 1, keepdims=False)
    other = swapped(lax.dynamic_index_in_dim(split, 1 - core, 1, keepdims=False), "c")
    first = jnp.where(core == 0, mine, other)
    second = jnp.where(core == 0, other, mine)
    return jnp.concatenate([first, second], axis=-1)


def summed_over_layer(partial_value):
    arrived = spread(partial_value.reshape(4, 2 * BS, BS), LAYER).reshape(2, 2, 2 * BS, BS)
    total = arrived.astype(jnp.float32).sum(axis=0)
    return jnp.concatenate([total[0], total[1]], axis=-1)


def on_device(
    root_values,
    root_columns,
    root_counts,
    fock_values,
    fock_columns,
    fock_counts,
    density_values,
    density_columns,
    density_counts,
):
    row, zh, core = (lax.axis_index(a) for a in ("row", "zh", "c"))
    target = row * 2 + core
    places = [
        jnp.stack([first, target]).astype(jnp.int32)
        for first in (zh * HALF, (1 - zh) * HALF, jnp.int32(0))
    ]

    def listed(*pairs):
        parts = [part for columns, counts in pairs for part in (columns[:, 0].T, counts.T)]
        own = jnp.concatenate(parts).reshape(-1)
        return own, swapped(own, "c")

    def pair(values):
        tiles = values[:, 0]
        return tiles, swapped(tiles, "c")

    def product(mat, metas, held, slab):
        def rows(place, count, dtype):
            return multiplied(mat, slab, metas, held, place, count, dtype)

        return rows

    def extraction(mat, metas, held):
        def rows(place, count, dtype):
            return extracted(mat, metas, held, place, count, dtype)

        return rows

    root = pair(root_values)
    root_metas = listed((root_columns, root_counts))
    root_slab = exchanged(extraction(0, root_metas, root), places)
    density = pair(density_values)
    fock = pair(fock_values)
    metas = listed((fock_columns, fock_counts), (density_columns, density_counts))
    density_slab = exchanged(extraction(1, metas, density), places)

    slab = gathered_x(gathered_z(root_slab))
    fock_inner = exchanged(product(0, metas, fock, slab), places)
    slab = gathered_x(gathered_z(density_slab))
    squared = exchanged(product(1, metas, density, slab), places)
    slab = gathered_x(gathered_z(fock_inner))
    fock_slab = exchanged(product(0, root_metas, root, slab), places)
    slab = gathered_x(gathered_z(squared))
    cubed_term = exchanged(product(1, metas, density, slab), places, jnp.float32)
    purified = 3.0 * squared.astype(jnp.float32) - 2.0 * cubed_term
    slab = gathered_x(gathered_z(fock_slab))
    outs = all_columns([fock_slab, purified.astype(jnp.bfloat16)])
    rows = product(1, metas, density, slab)
    energy = summed_over_layer(rows(places[2], RB, jnp.bfloat16))
    return outs[0], outs[1], energy.astype(jnp.bfloat16)


def solution(mesh):
    finer = Mesh(mesh.devices.reshape(mesh.shape["row"], 4, 4, 2, 2), ("row", *COL, *LAYER))
    specs = (P(COL, LAYER, None, None, None), P(COL, LAYER, None), P(COL, LAYER))

    return jax.shard_map(
        on_device,
        mesh=finer,
        in_specs=specs * 3,
        out_specs=(P((*COL, *LAYER), "row"),) * 3,
        check_vma=False,
    )
```

```python
import functools

import jax
import jax.numpy as jnp
from jax import lax
from jax.experimental import pallas as pl
from jax.experimental.pallas import tpu as pltpu
from jax.sharding import Mesh
from jax.sharding import PartitionSpec as P


BS = 128
KQ = 6
RB = 8
HALF = RB // 2
META = KQ + 1
VMEM = 12 << 20
SMALL = 4 << 20
COL = ("zl", "x")
LAYER = ("zh", "c")


def swapped(value, axis):
    return lax.ppermute(value, axis, [(0, 1), (1, 0)])


def spread(value, axis):
    return lax.all_to_all(value, axis, split_axis=0, concat_axis=0, tiled=True)


def extract_kernel(mat, own_meta, other_meta, place, own, other, sent, kept, found, sems):
    def slot(meta, row):
        at, hit = jnp.int32(0), jnp.int32(0)
        listed = meta[(mat * META + KQ) * RB + row]
        for k in range(KQ):
            here = (meta[(mat * META + k) * RB + row] == place[1]) & (k < listed)
            at = jnp.where(here, k, at)
            hit = jnp.where(here, 1, hit)
        return at, hit

    copies, hits = [], []
    for r in range(RB):
        row = (place[0] + r) & (RB - 1)
        for side, (meta, tiles) in enumerate(((own_meta, own), (other_meta, other))):
            at, hit = slot(meta, row)
            copy = pltpu.make_async_copy(tiles.at[row, at], found.at[r, side], sems.at[r, side])
            copy.start()
            copies.append(copy)
            hits.append(hit)
    for r in range(RB):
        copies[2 * r].wait()
        copies[2 * r + 1].wait()
        zero = jnp.zeros((BS, BS), found.dtype)
        tile = jnp.where(hits[2 * r] > 0, found[r, 0], zero)
        tile = jnp.where(hits[2 * r + 1] > 0, found[r, 1], tile)
        out = sent if r < HALF else kept
        out[r % HALF] = tile.astype(out.dtype)


def row_total(mat, row, metas, tiles, slab):
    left, right = [], []
    for side, meta in enumerate(metas):
        listed = meta[(mat * META + KQ) * RB + row]
        for k in range(KQ):
            j = meta[(mat * META + k) * RB + row]
            tile = tiles(side, k)
            left.append(jnp.where(k < listed, tile, jnp.zeros_like(tile)))
            right.append(slab[(((j >> 3) & 3) * 4 + (j >> 5)) * HALF + (j & 3)])
    return jnp.dot(
        jnp.concatenate(left, axis=1),
        jnp.concatenate(right, axis=0),
        preferred_element_type=jnp.float32,
    )


def product_kernel(mat, count, own_meta, other_meta, place, own, other, slab, out):
    for r in range(count):
        row = place[0] + r

        def tiles(side, k, row=row):
            return (own, other)[side][row, k]

        total = row_total(mat, row, (own_meta, other_meta), tiles, slab)
        out[r] = total.astype(out.dtype)


def halves_kernel(mat, own_meta, other_meta, place, own, other, slab, sent, kept, held, near, sems):
    slab_copy = pltpu.make_async_copy(slab, near, sems.at[2 * RB])
    slab_copy.start()
    copies = []
    for r in range(RB):
        row = (place[0] + r) & (RB - 1)
        for side, ref in enumerate((own, other)):
            to = held.at[r, pl.ds(side * KQ, KQ)]
            copy = pltpu.make_async_copy(ref.at[row], to, sems.at[2 * r + side])
            copy.start()
            copies.append(copy)
    slab_copy.wait()
    for r in range(RB):
        copies[2 * r].wait()
        copies[2 * r + 1].wait()
        row = (place[0] + r) & (RB - 1)

        def tiles(side, k, r=r):
            return held[r, side * KQ + k]

        total = row_total(mat, row, (own_meta, other_meta), tiles, near)
        out = sent if r < HALF else kept
        out[r % HALF] = total.astype(out.dtype)


def local_call(kernel, place, metas, operands, spaces, outs, scratch):
    rows = sum(out.shape[0] for out in outs)
    return pl.pallas_call(
        kernel,
        out_shape=outs,
        in_specs=[pl.BlockSpec(memory_space=pltpu.SMEM)] * 3
        + [pl.BlockSpec(memory_space=space) for space in spaces],
        out_specs=[pl.BlockSpec(memory_space=pltpu.VMEM) for _ in outs],
        scratch_shapes=scratch,
        compiler_params=pltpu.CompilerParams(vmem_limit_bytes=VMEM),
        cost_estimate=pl.CostEstimate(
            flops=2 * rows * 2 * KQ * BS * BS * BS,
            bytes_accessed=rows * 2 * KQ * BS * BS * 2,
            transcendentals=0,
        ),
    )(*metas, place, *operands)


def rows_of(count, dtype):
    return jax.ShapeDtypeStruct((count, BS, BS), dtype)


HALVES = (rows_of(HALF, jnp.bfloat16), rows_of(HALF, jnp.float32))


def in_hbm(value):
    return pltpu.with_memory_space_constraint(value, pltpu.HBM)


def extracted(mat, metas, held, places):
    scratch = [pltpu.VMEM((RB, 2, BS, BS), jnp.bfloat16), pltpu.SemaphoreType.DMA((RB, 2))]
    kernel = functools.partial(extract_kernel, mat)
    return local_call(kernel, places[1], metas, held, [pl.ANY] * 2, HALVES, scratch)


def halves(mat, metas, held, slab, places):
    scratch = [
        pltpu.VMEM((RB, 2 * KQ, BS, BS), jnp.bfloat16),
        pltpu.VMEM((64, BS, BS), jnp.bfloat16),
        pltpu.SemaphoreType.DMA((2 * RB + 1,)),
    ]
    kernel = functools.partial(halves_kernel, mat)
    operands = [*map(in_hbm, held), slab]
    spaces = [pltpu.HBM, pltpu.HBM, pl.ANY]
    return local_call(kernel, places[1], metas, operands, spaces, HALVES, scratch)


def multiplied(mat, metas, held, slab, place, count, dtype):
    kernel = functools.partial(product_kernel, mat, count)
    outs = (rows_of(count, dtype),)
    return local_call(kernel, place, metas, [*held, slab], [pltpu.VMEM] * 3, outs, [])[0]


def add_kernel(kept, arrived, out):
    out[...] = (kept[...] + arrived[...].astype(jnp.float32)).astype(out.dtype)


def copies_kernel(piece, out, sems):
    copies = [pltpu.make_async_copy(piece, out.at[i], sems.at[i]) for i in range(4)]
    for copy in copies:
        copy.start()
    for copy in copies:
        copy.wait()


def small_call(kernel, operands, shape, space, scratch, dtype=jnp.bfloat16):
    return pl.pallas_call(
        kernel,
        out_shape=jax.ShapeDtypeStruct(shape, dtype),
        in_specs=[pl.BlockSpec(memory_space=pltpu.VMEM) for _ in operands],
        out_specs=pl.BlockSpec(memory_space=space),
        scratch_shapes=scratch,
        compiler_params=pltpu.CompilerParams(vmem_limit_bytes=SMALL),
    )(*operands)


def exchanged(sent, kept, dtype=jnp.bfloat16):
    arrived = swapped(sent, "zh")
    kept = kept()
    return small_call(add_kernel, [kept, arrived], kept.shape, pltpu.VMEM, [], dtype)


def gathered_z(piece):
    return lax.all_gather(piece, "zl", axis=0, tiled=True)


def gathered_x(along_z):
    sems = [pltpu.SemaphoreType.DMA((4,))]
    copies = small_call(copies_kernel, [along_z], (4, *along_z.shape), pl.ANY, sems)
    return spread(copies, "x").reshape(-1, BS, BS)


def all_columns(pieces):
    core = lax.axis_index("c")
    split = jnp.stack(pieces).reshape(len(pieces), 2, 2 * BS, BS)
    mine = lax.dynamic_index_in_dim(split, core, 1, keepdims=False)
    other = swapped(lax.dynamic_index_in_dim(split, 1 - core, 1, keepdims=False), "c")
    first = jnp.where(core == 0, mine, other)
    second = jnp.where(core == 0, other, mine)
    return jnp.concatenate([first, second], axis=-1)


def summed_over_layer(partial_value):
    arrived = spread(partial_value.reshape(4, 2 * BS, BS), LAYER).reshape(2, 2, 2 * BS, BS)
    total = arrived.astype(jnp.float32).sum(axis=0)
    return jnp.concatenate([total[0], total[1]], axis=-1)


def on_device(
    root_values,
    root_columns,
    root_counts,
    fock_values,
    fock_columns,
    fock_counts,
    density_values,
    density_columns,
    density_counts,
):
    row, zh, core = (lax.axis_index(a) for a in ("row", "zh", "c"))
    target = row * 2 + core
    places = [
        jnp.stack([first, target]).astype(jnp.int32)
        for first in (zh * HALF, (1 - zh) * HALF, jnp.int32(0))
    ]

    def listed(*pairs):
        parts = [part for columns, counts in pairs for part in (columns[:, 0].T, counts.T)]
        own = jnp.concatenate(parts).reshape(-1)
        return own, swapped(own, "c")

    def pair(values):
        tiles = values[:, 0]
        return tiles, swapped(tiles, "c")

    def at_once(pieces):
        return exchanged(pieces[0], lambda: pieces[1])

    def in_turn(mat, held, slab, dtype=jnp.bfloat16):
        sent = multiplied(mat, metas, held, slab, places[1], HALF, jnp.bfloat16)
        kept = functools.partial(multiplied, mat, metas, held, slab, places[0], HALF, jnp.float32)
        return exchanged(sent, kept, dtype)

    root = pair(root_values)
    root_metas = listed((root_columns, root_counts))
    root_slab = at_once(extracted(0, root_metas, [*map(in_hbm, root)], places))
    density = pair(density_values)
    fock = pair(fock_values)
    metas = listed(
        (fock_columns, fock_counts), (density_columns, density_counts), (root_columns, root_counts)
    )
    density_slab = at_once(extracted(1, metas, density, places))

    slab = gathered_x(gathered_z(root_slab))
    fock_inner = at_once(halves(0, metas, fock, slab, places))
    slab = gathered_x(gathered_z(density_slab))
    squared = in_turn(1, density, slab)
    slab = gathered_x(gathered_z(fock_inner))
    fock_slab = at_once(halves(2, metas, root, slab, places))
    slab = gathered_x(gathered_z(squared))
    cubed_term = in_turn(1, density, slab, jnp.float32)
    purified = 3.0 * squared.astype(jnp.float32) - 2.0 * cubed_term
    slab = gathered_x(gathered_z(fock_slab))
    outs = all_columns([fock_slab, purified.astype(jnp.bfloat16)])
    rows = multiplied(1, metas, density, slab, places[2], RB, jnp.bfloat16)
    energy = summed_over_layer(rows)
    return outs[0], outs[1], energy.astype(jnp.bfloat16)


def solution(mesh):
    finer = Mesh(mesh.devices.reshape(mesh.shape["row"], 4, 4, 2, 2), ("row", *COL, *LAYER))
    specs = (P(COL, LAYER, None, None, None), P(COL, LAYER, None), P(COL, LAYER))

    return jax.shard_map(
        on_device,
        mesh=finer,
        in_specs=specs * 3,
        out_specs=(P((*COL, *LAYER), "row"),) * 3,
        check_vma=False,
    )
```

```python
import functools

import jax
import jax.numpy as jnp
from jax import lax
from jax.experimental import pallas as pl
from jax.experimental.pallas import tpu as pltpu
from jax.sharding import Mesh
from jax.sharding import PartitionSpec as P


BS = 128
KQ = 6
RB = 8
HALF = RB // 2
META = KQ + 1
VMEM = 12 << 20
SMALL = 4 << 20
COL = ("zl", "x")
LAYER = ("zh", "c")


def swapped(value, axis):
    return lax.ppermute(value, axis, [(0, 1), (1, 0)])


def spread(value, axis):
    return lax.all_to_all(value, axis, split_axis=0, concat_axis=0, tiled=True)


def extract_kernel(mat, own_meta, other_meta, place, own, other, sent, kept, found, sems):
    def slot(meta, row):
        at, hit = jnp.int32(0), jnp.int32(0)
        listed = meta[mat * META + KQ, 0, row]
        for k in range(KQ):
            here = (meta[mat * META + k, 0, row] == place[1]) & (k < listed)
            at = jnp.where(here, k, at)
            hit = jnp.where(here, 1, hit)
        return at, hit

    copies, hits = [], []
    for r in range(RB):
        row = (place[0] + r) & (RB - 1)
        for side, (meta, tiles) in enumerate(((own_meta, own), (other_meta, other))):
            at, hit = slot(meta, row)
            copy = pltpu.make_async_copy(tiles.at[row, at], found.at[r, side], sems.at[r, side])
            copy.start()
            copies.append(copy)
            hits.append(hit)
    for r in range(RB):
        copies[2 * r].wait()
        copies[2 * r + 1].wait()
        zero = jnp.zeros((BS, BS), found.dtype)
        tile = jnp.where(hits[2 * r] > 0, found[r, 0], zero)
        tile = jnp.where(hits[2 * r + 1] > 0, found[r, 1], tile)
        out = sent if r < HALF else kept
        out[r % HALF] = tile.astype(out.dtype)


def row_total(mat, row, metas, tiles, slab):
    left, right = [], []
    for side, meta in enumerate(metas):
        listed = meta[mat * META + KQ, 0, row]
        for k in range(KQ):
            j = meta[mat * META + k, 0, row]
            tile = tiles(side, k)
            left.append(jnp.where(k < listed, tile, jnp.zeros_like(tile)))
            right.append(slab[(((j >> 3) & 3) * 4 + (j >> 5)) * HALF + (j & 3)])
    return jnp.dot(
        jnp.concatenate(left, axis=1),
        jnp.concatenate(right, axis=0),
        preferred_element_type=jnp.float32,
    )


def product_kernel(mat, count, own_meta, other_meta, place, own, other, slab, out):
    for r in range(count):
        row = place[0] + r

        def tiles(side, k, row=row):
            return (own, other)[side][row, k]

        total = row_total(mat, row, (own_meta, other_meta), tiles, slab)
        out[r] = total.astype(out.dtype)


def halves_kernel(mat, own_meta, other_meta, place, own, other, slab, sent, kept, held, near, sems):
    slab_copy = pltpu.make_async_copy(slab, near, sems.at[2 * RB])
    slab_copy.start()
    copies = []
    for r in range(RB):
        row = (place[0] + r) & (RB - 1)
        for side, ref in enumerate((own, other)):
            to = held.at[r, pl.ds(side * KQ, KQ)]
            copy = pltpu.make_async_copy(ref.at[row], to, sems.at[2 * r + side])
            copy.start()
            copies.append(copy)
    slab_copy.wait()
    for r in range(RB):
        copies[2 * r].wait()
        copies[2 * r + 1].wait()
        row = (place[0] + r) & (RB - 1)

        def tiles(side, k, r=r):
            return held[r, side * KQ + k]

        total = row_total(mat, row, (own_meta, other_meta), tiles, near)
        out = sent if r < HALF else kept
        out[r % HALF] = total.astype(out.dtype)


def local_call(kernel, place, metas, operands, spaces, outs, scratch):
    rows = sum(out.shape[0] for out in outs)
    return pl.pallas_call(
        kernel,
        out_shape=outs,
        in_specs=[pl.BlockSpec(memory_space=pltpu.SMEM)] * 3
        + [pl.BlockSpec(memory_space=space) for space in spaces],
        out_specs=[pl.BlockSpec(memory_space=pltpu.VMEM) for _ in outs],
        scratch_shapes=scratch,
        compiler_params=pltpu.CompilerParams(vmem_limit_bytes=VMEM),
        cost_estimate=pl.CostEstimate(
            flops=2 * rows * 2 * KQ * BS * BS * BS,
            bytes_accessed=rows * 2 * KQ * BS * BS * 2,
            transcendentals=0,
        ),
    )(*metas, place, *operands)


def rows_of(count, dtype):
    return jax.ShapeDtypeStruct((count, BS, BS), dtype)


HALVES = (rows_of(HALF, jnp.bfloat16), rows_of(HALF, jnp.float32))


def in_hbm(value):
    return pltpu.with_memory_space_constraint(value, pltpu.HBM)


def extracted(mat, metas, held, places):
    scratch = [pltpu.VMEM((RB, 2, BS, BS), jnp.bfloat16), pltpu.SemaphoreType.DMA((RB, 2))]
    kernel = functools.partial(extract_kernel, mat)
    return local_call(kernel, places[1], metas, held, [pl.ANY] * 2, HALVES, scratch)


def halves(mat, metas, held, slab, places):
    scratch = [
        pltpu.VMEM((RB, 2 * KQ, BS, BS), jnp.bfloat16),
        pltpu.VMEM((64, BS, BS), jnp.bfloat16),
        pltpu.SemaphoreType.DMA((2 * RB + 1,)),
    ]
    kernel = functools.partial(halves_kernel, mat)
    operands = [*map(in_hbm, held), slab]
    spaces = [pltpu.HBM, pltpu.HBM, pl.ANY]
    return local_call(kernel, places[1], metas, operands, spaces, HALVES, scratch)


def multiplied(mat, metas, held, slab, place, count, dtype):
    kernel = functools.partial(product_kernel, mat, count)
    outs = (rows_of(count, dtype),)
    return local_call(kernel, place, metas, [*held, slab], [pltpu.VMEM] * 3, outs, [])[0]


def add_kernel(kept, arrived, out):
    out[...] = (kept[...] + arrived[...].astype(jnp.float32)).astype(out.dtype)


def copies_kernel(piece, out, sems):
    copies = [pltpu.make_async_copy(piece, out.at[i], sems.at[i]) for i in range(4)]
    for copy in copies:
        copy.start()
    for copy in copies:
        copy.wait()


def small_call(kernel, operands, shape, space, scratch, dtype=jnp.bfloat16):
    return pl.pallas_call(
        kernel,
        out_shape=jax.ShapeDtypeStruct(shape, dtype),
        in_specs=[pl.BlockSpec(memory_space=pltpu.VMEM) for _ in operands],
        out_specs=pl.BlockSpec(memory_space=space),
        scratch_shapes=scratch,
        compiler_params=pltpu.CompilerParams(vmem_limit_bytes=SMALL),
    )(*operands)


def exchanged(sent, kept, dtype=jnp.bfloat16):
    arrived = swapped(sent, "zh")
    kept = kept()
    return small_call(add_kernel, [kept, arrived], kept.shape, pltpu.VMEM, [], dtype)


def gathered_z(piece):
    return lax.all_gather(piece, "zl", axis=0, tiled=True)


def gathered_x(along_z):
    sems = [pltpu.SemaphoreType.DMA((4,))]
    copies = small_call(copies_kernel, [along_z], (4, *along_z.shape), pl.ANY, sems)
    return spread(copies, "x").reshape(-1, BS, BS)


def all_columns(pieces):
    core = lax.axis_index("c")
    split = jnp.stack(pieces).reshape(len(pieces), 2, 2 * BS, BS)
    mine = lax.dynamic_index_in_dim(split, core, 1, keepdims=False)
    other = swapped(lax.dynamic_index_in_dim(split, 1 - core, 1, keepdims=False), "c")
    first = jnp.where(core == 0, mine, other)
    second = jnp.where(core == 0, other, mine)
    return jnp.concatenate([first, second], axis=-1)


def summed_over_layer(partial_value):
    arrived = spread(partial_value.reshape(4, 2 * BS, BS), LAYER).reshape(2, 2, 2 * BS, BS)
    total = arrived.astype(jnp.float32).sum(axis=0)
    return jnp.concatenate([total[0], total[1]], axis=-1)


def on_device(
    root_values,
    root_columns,
    root_counts,
    fock_values,
    fock_columns,
    fock_counts,
    density_values,
    density_columns,
    density_counts,
):
    row, zh, core = (lax.axis_index(a) for a in ("row", "zh", "c"))
    target = row * 2 + core
    places = [
        jnp.stack([first, target]).astype(jnp.int32)
        for first in (zh * HALF, (1 - zh) * HALF, jnp.int32(0))
    ]

    def listed(*pairs):
        parts = []
        for columns, counts in pairs:
            parts += [columns.transpose(2, 1, 0), counts.T[:, None]]
        own = jnp.concatenate(parts)
        return own, swapped(own, "c")

    def pair(values):
        tiles = values[:, 0]
        return tiles, swapped(tiles, "c")

    def at_once(pieces):
        return exchanged(pieces[0], lambda: pieces[1])

    def in_turn(mat, held, slab, dtype=jnp.bfloat16):
        sent = multiplied(mat, metas, held, slab, places[1], HALF, jnp.bfloat16)
        kept = functools.partial(multiplied, mat, metas, held, slab, places[0], HALF, jnp.float32)
        return exchanged(sent, kept, dtype)

    root = pair(root_values)
    root_metas = listed((root_columns, root_counts))
    root_slab = at_once(extracted(0, root_metas, [*map(in_hbm, root)], places))
    density = pair(density_values)
    fock = pair(fock_values)
    metas = listed(
        (fock_columns, fock_counts), (density_columns, density_counts), (root_columns, root_counts)
    )
    density_slab = at_once(extracted(1, metas, density, places))

    slab = gathered_x(gathered_z(root_slab))
    fock_inner = at_once(halves(0, metas, fock, slab, places))
    slab = gathered_x(gathered_z(density_slab))
    squared = in_turn(1, density, slab)
    slab = gathered_x(gathered_z(fock_inner))
    fock_slab = at_once(halves(2, metas, root, slab, places))
    slab = gathered_x(gathered_z(squared))
    cubed_term = in_turn(1, density, slab, jnp.float32)
    purified = 3.0 * squared.astype(jnp.float32) - 2.0 * cubed_term
    slab = gathered_x(gathered_z(fock_slab))
    outs = all_columns([fock_slab, purified.astype(jnp.bfloat16)])
    rows = multiplied(1, metas, density, slab, places[2], RB, jnp.bfloat16)
    energy = summed_over_layer(rows)
    return outs[0], outs[1], energy.astype(jnp.bfloat16)


def solution(mesh):
    finer = Mesh(mesh.devices.reshape(mesh.shape["row"], 4, 4, 2, 2), ("row", *COL, *LAYER))
    specs = (P(COL, LAYER, None, None, None), P(COL, LAYER, None), P(COL, LAYER))

    return jax.shard_map(
        on_device,
        mesh=finer,
        in_specs=specs * 3,
        out_specs=(P((*COL, *LAYER), "row"),) * 3,
        check_vma=False,
    )
```

```python
import functools

import jax
import jax.numpy as jnp
from jax import lax
from jax.experimental import pallas as pl
from jax.experimental.pallas import tpu as pltpu
from jax.sharding import Mesh
from jax.sharding import PartitionSpec as P


BS = 128
KQ = 6
RB = 8
HALF = RB // 2
META = KQ + 1
VMEM = 12 << 20
SMALL = 4 << 20
COL = ("zl", "x")
LAYER = ("zh", "c")


def swapped(value, axis):
    return lax.ppermute(value, axis, [(0, 1), (1, 0)])


def spread(value, axis):
    return lax.all_to_all(value, axis, split_axis=0, concat_axis=0, tiled=True)


def extract_kernel(mat, own_meta, other_meta, place, own, other, sent, kept, found, sems):
    def slot(meta, row):
        at, hit = jnp.int32(0), jnp.int32(0)
        listed = meta[mat * META + KQ, 0, row]
        for k in range(KQ):
            here = (meta[mat * META + k, 0, row] == place[1]) & (k < listed)
            at = jnp.where(here, k, at)
            hit = jnp.where(here, 1, hit)
        return at, hit

    copies, hits = [], []
    for r in range(RB):
        row = (place[0] + r) & (RB - 1)
        for side, (meta, tiles) in enumerate(((own_meta, own), (other_meta, other))):
            at, hit = slot(meta, row)
            copy = pltpu.make_async_copy(tiles.at[row, at], found.at[r, side], sems.at[r, side])
            copy.start()
            copies.append(copy)
            hits.append(hit)
    for r in range(RB):
        copies[2 * r].wait()
        copies[2 * r + 1].wait()
        zero = jnp.zeros((BS, BS), found.dtype)
        tile = jnp.where(hits[2 * r] > 0, found[r, 0], zero)
        tile = jnp.where(hits[2 * r + 1] > 0, found[r, 1], tile)
        out = sent if r < HALF else kept
        out[r % HALF] = tile.astype(out.dtype)


def row_total(mat, row, metas, tiles, slab):
    left, right = [], []
    for side, meta in enumerate(metas):
        listed = meta[mat * META + KQ, 0, row]
        for k in range(KQ):
            j = meta[mat * META + k, 0, row]
            tile = tiles(side, k)
            left.append(jnp.where(k < listed, tile, jnp.zeros_like(tile)))
            right.append(slab[(((j >> 3) & 3) * 4 + (j >> 5)) * HALF + (j & 3)])
    return jnp.dot(
        jnp.concatenate(left, axis=1),
        jnp.concatenate(right, axis=0),
        preferred_element_type=jnp.float32,
    )


def product_kernel(mat, count, own_meta, other_meta, place, own, other, slab, out):
    for r in range(count):
        row = place[0] + r

        def tiles(side, k, row=row):
            return (own, other)[side][row, k]

        total = row_total(mat, row, (own_meta, other_meta), tiles, slab)
        out[r] = total.astype(out.dtype)


def fetched_kernel(mat, own_meta, other_meta, place, own, other, slab, out, held, near, sems):
    slab_copy = pltpu.make_async_copy(slab, near, sems.at[2 * HALF])
    slab_copy.start()
    copies = []
    for r in range(HALF):
        for side, ref in enumerate((own, other)):
            to = held.at[r, pl.ds(side * KQ, KQ)]
            copy = pltpu.make_async_copy(ref.at[place[0] + r], to, sems.at[2 * r + side])
            copy.start()
            copies.append(copy)
    slab_copy.wait()
    for r in range(HALF):
        copies[2 * r].wait()
        copies[2 * r + 1].wait()

        def tiles(side, k, r=r):
            return held[r, side * KQ + k]

        total = row_total(mat, place[0] + r, (own_meta, other_meta), tiles, near)
        out[r] = total.astype(out.dtype)


def local_call(kernel, place, metas, operands, spaces, outs, scratch):
    rows = sum(out.shape[0] for out in outs)
    return pl.pallas_call(
        kernel,
        out_shape=outs,
        in_specs=[pl.BlockSpec(memory_space=pltpu.SMEM)] * 3
        + [pl.BlockSpec(memory_space=space) for space in spaces],
        out_specs=[pl.BlockSpec(memory_space=pltpu.VMEM) for _ in outs],
        scratch_shapes=scratch,
        compiler_params=pltpu.CompilerParams(vmem_limit_bytes=VMEM),
        cost_estimate=pl.CostEstimate(
            flops=2 * rows * 2 * KQ * BS * BS * BS,
            bytes_accessed=rows * 2 * KQ * BS * BS * 2,
            transcendentals=0,
        ),
    )(*metas, place, *operands)


def rows_of(count, dtype):
    return jax.ShapeDtypeStruct((count, BS, BS), dtype)


HALVES = (rows_of(HALF, jnp.bfloat16),) * 2


def in_hbm(value):
    return pltpu.with_memory_space_constraint(value, pltpu.HBM)


def extracted(mat, metas, held, places):
    scratch = [pltpu.VMEM((RB, 2, BS, BS), jnp.bfloat16), pltpu.SemaphoreType.DMA((RB, 2))]
    kernel = functools.partial(extract_kernel, mat)
    return local_call(kernel, places[1], metas, held, [pl.ANY] * 2, HALVES, scratch)


def fetched(mat, metas, held, slab, place, count, dtype):
    scratch = [
        pltpu.VMEM((count, 2 * KQ, BS, BS), jnp.bfloat16),
        pltpu.VMEM((64, BS, BS), jnp.bfloat16),
        pltpu.SemaphoreType.DMA((2 * count + 1,)),
    ]
    kernel = functools.partial(fetched_kernel, mat)
    operands = [*map(in_hbm, held), slab]
    spaces = [pltpu.HBM, pltpu.HBM, pl.ANY]
    return local_call(kernel, place, metas, operands, spaces, (rows_of(count, dtype),), scratch)[0]


def multiplied(mat, metas, held, slab, place, count, dtype):
    kernel = functools.partial(product_kernel, mat, count)
    outs = (rows_of(count, dtype),)
    return local_call(kernel, place, metas, [*held, slab], [pltpu.VMEM] * 3, outs, [])[0]


def add_kernel(kept, arrived, out):
    out[...] = (kept[...] + arrived[...].astype(jnp.float32)).astype(out.dtype)


def copies_kernel(piece, out, sems):
    copies = [pltpu.make_async_copy(piece, out.at[i], sems.at[i]) for i in range(4)]
    for copy in copies:
        copy.start()
    for copy in copies:
        copy.wait()


def small_call(kernel, operands, shape, space, scratch, dtype=jnp.bfloat16):
    return pl.pallas_call(
        kernel,
        out_shape=jax.ShapeDtypeStruct(shape, dtype),
        in_specs=[pl.BlockSpec(memory_space=pltpu.VMEM) for _ in operands],
        out_specs=pl.BlockSpec(memory_space=space),
        scratch_shapes=scratch,
        compiler_params=pltpu.CompilerParams(vmem_limit_bytes=SMALL),
    )(*operands)


def exchanged(sent, kept, dtype=jnp.bfloat16):
    arrived = swapped(sent, "zh")
    kept = kept()
    return small_call(add_kernel, [kept, arrived], kept.shape, pltpu.VMEM, [], dtype)


def gathered_z(piece):
    return lax.all_gather(piece, "zl", axis=0, tiled=True)


def gathered_x(along_z):
    sems = [pltpu.SemaphoreType.DMA((4,))]
    copies = small_call(copies_kernel, [along_z], (4, *along_z.shape), pl.ANY, sems)
    return spread(copies, "x").reshape(-1, BS, BS)


def all_columns(pieces):
    core = lax.axis_index("c")
    split = jnp.stack(pieces).reshape(len(pieces), 2, 2 * BS, BS)
    mine = lax.dynamic_index_in_dim(split, core, 1, keepdims=False)
    other = swapped(lax.dynamic_index_in_dim(split, 1 - core, 1, keepdims=False), "c")
    first = jnp.where(core == 0, mine, other)
    second = jnp.where(core == 0, other, mine)
    return jnp.concatenate([first, second], axis=-1)


def summed_over_layer(partial_value):
    arrived = spread(partial_value.reshape(4, 2 * BS, BS), LAYER).reshape(2, 2, 2 * BS, BS)
    total = arrived.astype(jnp.float32).sum(axis=0)
    return jnp.concatenate([total[0], total[1]], axis=-1)


def on_device(
    root_values,
    root_columns,
    root_counts,
    fock_values,
    fock_columns,
    fock_counts,
    density_values,
    density_columns,
    density_counts,
):
    row, zh, core = (lax.axis_index(a) for a in ("row", "zh", "c"))
    target = row * 2 + core
    places = [
        jnp.stack([first, target]).astype(jnp.int32)
        for first in (zh * HALF, (1 - zh) * HALF, jnp.int32(0))
    ]

    def listed(*pairs):
        parts = []
        for columns, counts in pairs:
            parts += [columns.transpose(2, 1, 0), counts.T[:, None]]
        own = jnp.concatenate(parts)
        return own, swapped(own, "c")

    def pair(values):
        tiles = values[:, 0]
        return tiles, swapped(tiles, "c")

    def at_once(pieces):
        return exchanged(pieces[0], lambda: pieces[1])

    def in_turn(rows, mat, held, slab, dtype=jnp.bfloat16):
        sent = rows(mat, metas, held, slab, places[1], HALF, jnp.bfloat16)
        kept = functools.partial(rows, mat, metas, held, slab, places[0], HALF, jnp.float32)
        return exchanged(sent, kept, dtype)

    root = pair(root_values)
    root_metas = listed((root_columns, root_counts))
    root_slab = at_once(extracted(0, root_metas, [*map(in_hbm, root)], places))
    density = pair(density_values)
    fock = pair(fock_values)
    metas = listed(
        (fock_columns, fock_counts), (density_columns, density_counts), (root_columns, root_counts)
    )
    density_slab = at_once(extracted(1, metas, density, places))

    slab = gathered_x(gathered_z(root_slab))
    fock_inner = in_turn(fetched, 0, fock, slab)
    slab = gathered_x(gathered_z(density_slab))
    squared = in_turn(multiplied, 1, density, slab)
    slab = gathered_x(gathered_z(fock_inner))
    fock_slab = in_turn(fetched, 2, root, slab)
    slab = gathered_x(gathered_z(squared))
    cubed_term = in_turn(multiplied, 1, density, slab, jnp.float32)
    purified = 3.0 * squared.astype(jnp.float32) - 2.0 * cubed_term
    slab = gathered_x(gathered_z(fock_slab))
    outs = all_columns([fock_slab, purified.astype(jnp.bfloat16)])
    rows = multiplied(1, metas, density, slab, places[2], RB, jnp.bfloat16)
    energy = summed_over_layer(rows)
    return outs[0], outs[1], energy.astype(jnp.bfloat16)


def solution(mesh):
    finer = Mesh(mesh.devices.reshape(mesh.shape["row"], 4, 4, 2, 2), ("row", *COL, *LAYER))
    specs = (P(COL, LAYER, None, None, None), P(COL, LAYER, None), P(COL, LAYER))

    return jax.shard_map(
        on_device,
        mesh=finer,
        in_specs=specs * 3,
        out_specs=(P((*COL, *LAYER), "row"),) * 3,
        check_vma=False,
    )
```

```python
import functools

import jax
import jax.numpy as jnp
from jax import lax
from jax.experimental import pallas as pl
from jax.experimental.pallas import tpu as pltpu
from jax.sharding import Mesh
from jax.sharding import PartitionSpec as P


BS = 128
KQ = 6
RB = 8
HALF = RB // 2
META = KQ + 1
VMEM = 12 << 20
SMALL = 4 << 20
COL = ("zl", "x")
LAYER = ("zh", "c")


def swapped(value, axis):
    return lax.ppermute(value, axis, [(0, 1), (1, 0)])


def spread(value, axis):
    return lax.all_to_all(value, axis, split_axis=0, concat_axis=0, tiled=True)


def extract_kernel(mat, own_meta, other_meta, place, own, other, out, found, sems):
    def slot(meta, row):
        at, hit = jnp.int32(0), jnp.int32(0)
        listed = meta[mat * META + KQ, 0, row]
        for k in range(KQ):
            here = (meta[mat * META + k, 0, row] == place[1]) & (k < listed)
            at = jnp.where(here, k, at)
            hit = jnp.where(here, 1, hit)
        return at, hit

    copies, hits = [], []
    for r in range(HALF):
        row = place[0] + r
        for side, (meta, tiles) in enumerate(((own_meta, own), (other_meta, other))):
            at, hit = slot(meta, row)
            copy = pltpu.make_async_copy(tiles.at[row, at], found.at[r, side], sems.at[r, side])
            copy.start()
            copies.append(copy)
            hits.append(hit)
    for r in range(HALF):
        copies[2 * r].wait()
        copies[2 * r + 1].wait()
        zero = jnp.zeros((BS, BS), found.dtype)
        tile = jnp.where(hits[2 * r] > 0, found[r, 0], zero)
        out[r] = jnp.where(hits[2 * r + 1] > 0, found[r, 1], tile)


def row_total(mat, row, metas, tiles, slab):
    left, right = [], []
    for side, meta in enumerate(metas):
        listed = meta[mat * META + KQ, 0, row]
        for k in range(KQ):
            j = meta[mat * META + k, 0, row]
            tile = tiles(side, k)
            left.append(jnp.where(k < listed, tile, jnp.zeros_like(tile)))
            right.append(slab[(((j >> 3) & 3) * 4 + (j >> 5)) * HALF + (j & 3)])
    return jnp.dot(
        jnp.concatenate(left, axis=1),
        jnp.concatenate(right, axis=0),
        preferred_element_type=jnp.float32,
    )


def product_kernel(mat, count, own_meta, other_meta, place, own, other, slab, out):
    for r in range(count):
        row = place[0] + r

        def tiles(side, k, row=row):
            return (own, other)[side][row, k]

        total = row_total(mat, row, (own_meta, other_meta), tiles, slab)
        out[r] = total.astype(out.dtype)


def fetched_kernel(mat, own_meta, other_meta, place, own, other, slab, out, held, near, sems):
    slab_copy = pltpu.make_async_copy(slab, near, sems.at[2 * HALF])
    slab_copy.start()
    copies = []
    for r in range(HALF):
        for side, ref in enumerate((own, other)):
            to = held.at[r, pl.ds(side * KQ, KQ)]
            copy = pltpu.make_async_copy(ref.at[place[0] + r], to, sems.at[2 * r + side])
            copy.start()
            copies.append(copy)
    slab_copy.wait()
    for r in range(HALF):
        copies[2 * r].wait()
        copies[2 * r + 1].wait()

        def tiles(side, k, r=r):
            return held[r, side * KQ + k]

        total = row_total(mat, place[0] + r, (own_meta, other_meta), tiles, near)
        out[r] = total.astype(out.dtype)


def local_call(kernel, place, metas, operands, spaces, outs, scratch):
    rows = sum(out.shape[0] for out in outs)
    return pl.pallas_call(
        kernel,
        out_shape=outs,
        in_specs=[pl.BlockSpec(memory_space=pltpu.SMEM)] * 3
        + [pl.BlockSpec(memory_space=space) for space in spaces],
        out_specs=[pl.BlockSpec(memory_space=pltpu.VMEM) for _ in outs],
        scratch_shapes=scratch,
        compiler_params=pltpu.CompilerParams(vmem_limit_bytes=VMEM),
        cost_estimate=pl.CostEstimate(
            flops=2 * rows * 2 * KQ * BS * BS * BS,
            bytes_accessed=rows * 2 * KQ * BS * BS * 2,
            transcendentals=0,
        ),
    )(*metas, place, *operands)


def rows_of(count, dtype):
    return jax.ShapeDtypeStruct((count, BS, BS), dtype)


def in_hbm(value):
    return pltpu.with_memory_space_constraint(value, pltpu.HBM)


def extracted(mat, metas, held, place):
    scratch = [pltpu.VMEM((HALF, 2, BS, BS), jnp.bfloat16), pltpu.SemaphoreType.DMA((HALF, 2))]
    kernel = functools.partial(extract_kernel, mat)
    outs = (rows_of(HALF, jnp.bfloat16),)
    return local_call(kernel, place, metas, held, [pl.ANY] * 2, outs, scratch)[0]


def fetched(mat, metas, held, slab, place, count, dtype):
    scratch = [
        pltpu.VMEM((count, 2 * KQ, BS, BS), jnp.bfloat16),
        pltpu.VMEM((64, BS, BS), jnp.bfloat16),
        pltpu.SemaphoreType.DMA((2 * count + 1,)),
    ]
    kernel = functools.partial(fetched_kernel, mat)
    operands = [*map(in_hbm, held), slab]
    spaces = [pltpu.HBM, pltpu.HBM, pl.ANY]
    return local_call(kernel, place, metas, operands, spaces, (rows_of(count, dtype),), scratch)[0]


def multiplied(mat, metas, held, slab, place, count, dtype):
    kernel = functools.partial(product_kernel, mat, count)
    outs = (rows_of(count, dtype),)
    return local_call(kernel, place, metas, [*held, slab], [pltpu.VMEM] * 3, outs, [])[0]


def add_kernel(kept, arrived, out):
    out[...] = (kept[...] + arrived[...].astype(jnp.float32)).astype(out.dtype)


def copies_kernel(piece, out, sems):
    copies = [pltpu.make_async_copy(piece, out.at[i], sems.at[i]) for i in range(4)]
    for copy in copies:
        copy.start()
    for copy in copies:
        copy.wait()


def small_call(kernel, operands, shape, space, scratch, dtype=jnp.bfloat16):
    return pl.pallas_call(
        kernel,
        out_shape=jax.ShapeDtypeStruct(shape, dtype),
        in_specs=[pl.BlockSpec(memory_space=pltpu.VMEM) for _ in operands],
        out_specs=pl.BlockSpec(memory_space=space),
        scratch_shapes=scratch,
        compiler_params=pltpu.CompilerParams(vmem_limit_bytes=SMALL),
    )(*operands)


def exchanged(sent, kept, dtype=jnp.bfloat16):
    arrived = swapped(sent, "zh")
    kept = kept()
    return small_call(add_kernel, [kept, arrived], kept.shape, pltpu.VMEM, [], dtype)


def gathered_z(piece):
    return lax.all_gather(piece, "zl", axis=0, tiled=True)


def gathered_x(along_z):
    sems = [pltpu.SemaphoreType.DMA((4,))]
    copies = small_call(copies_kernel, [along_z], (4, *along_z.shape), pl.ANY, sems)
    return spread(copies, "x").reshape(-1, BS, BS)


def all_columns(pieces):
    core = lax.axis_index("c")
    split = jnp.stack(pieces).reshape(len(pieces), 2, 2 * BS, BS)
    mine = lax.dynamic_index_in_dim(split, core, 1, keepdims=False)
    other = swapped(lax.dynamic_index_in_dim(split, 1 - core, 1, keepdims=False), "c")
    first = jnp.where(core == 0, mine, other)
    second = jnp.where(core == 0, other, mine)
    return jnp.concatenate([first, second], axis=-1)


def summed_over_layer(partial_value):
    arrived = spread(partial_value.reshape(4, 2 * BS, BS), LAYER).reshape(2, 2, 2 * BS, BS)
    total = arrived.astype(jnp.float32).sum(axis=0)
    return jnp.concatenate([total[0], total[1]], axis=-1)


def on_device(
    root_values,
    root_columns,
    root_counts,
    fock_values,
    fock_columns,
    fock_counts,
    density_values,
    density_columns,
    density_counts,
):
    row, zh, core = (lax.axis_index(a) for a in ("row", "zh", "c"))
    target = row * 2 + core
    places = [
        jnp.stack([first, target]).astype(jnp.int32)
        for first in (zh * HALF, (1 - zh) * HALF, jnp.int32(0))
    ]

    def listed(*pairs):
        parts = []
        for columns, counts in pairs:
            parts += [columns.transpose(2, 1, 0), counts.T[:, None]]
        own = jnp.concatenate(parts)
        return own, swapped(own, "c")

    def pair(values):
        tiles = values[:, 0]
        return tiles, swapped(tiles, "c")

    def extraction(mat, metas, held):
        sent = extracted(mat, metas, held, places[1])
        return exchanged(sent, lambda: extracted(mat, metas, held, places[0]))

    def in_turn(rows, mat, held, slab, dtype=jnp.bfloat16):
        sent = rows(mat, metas, held, slab, places[1], HALF, jnp.bfloat16)
        kept = functools.partial(rows, mat, metas, held, slab, places[0], HALF, jnp.float32)
        return exchanged(sent, kept, dtype)

    root = pair(root_values)
    root_metas = listed((root_columns, root_counts))
    root_slab = extraction(0, root_metas, [*map(in_hbm, root)])
    density = pair(density_values)
    fock = pair(fock_values)
    metas = listed(
        (fock_columns, fock_counts), (density_columns, density_counts), (root_columns, root_counts)
    )
    density_slab = extraction(1, metas, density)

    slab = gathered_x(gathered_z(root_slab))
    fock_inner = in_turn(fetched, 0, fock, slab)
    slab = gathered_x(gathered_z(density_slab))
    squared = in_turn(multiplied, 1, density, slab)
    slab = gathered_x(gathered_z(fock_inner))
    fock_slab = in_turn(fetched, 2, root, slab)
    slab = gathered_x(gathered_z(squared))
    cubed_term = in_turn(multiplied, 1, density, slab, jnp.float32)
    purified = 3.0 * squared.astype(jnp.float32) - 2.0 * cubed_term
    slab = gathered_x(gathered_z(fock_slab))
    outs = all_columns([fock_slab, purified.astype(jnp.bfloat16)])
    rows = multiplied(1, metas, density, slab, places[2], RB, jnp.bfloat16)
    energy = summed_over_layer(rows)
    return outs[0], outs[1], energy.astype(jnp.bfloat16)


def solution(mesh):
    finer = Mesh(mesh.devices.reshape(mesh.shape["row"], 4, 4, 2, 2), ("row", *COL, *LAYER))
    specs = (P(COL, LAYER, None, None, None), P(COL, LAYER, None), P(COL, LAYER))

    return jax.shard_map(
        on_device,
        mesh=finer,
        in_specs=specs * 3,
        out_specs=(P((*COL, *LAYER), "row"),) * 3,
        check_vma=False,
    )
```
